128 devices in a mesh: ty: 8 (over x, core), tx: 16 (over y, z).
Axes of the slice: x: 4, y: 4, z: 4, core: 2. Of those that a mesh axis runs over, the one named last changes fastest.
Arguments:
- gaussians: float32 [12288, 59, 128], P(('ty', 'tx')), may hold values from -18 to 22, as said below
- tile_lists: int32 [8, 16, 24], P('ty', 'tx'), may hold values from 0 to 12287, as said below
- tile_counts: int32 [8, 16], P('ty', 'tx'), may hold values from 3 to 24, as said below
- depth_order: int32 [12288], replicated, may hold values from 0 to 12287, as said below
- target: float32 [3, 256, 512], P(None, 'ty', 'tx'), may hold values from 0 to 1
Outputs:
- gaussian_grads: float32 [12288, 59, 128], P(('ty', 'tx'))
- loss: float32 [], replicated
The draws below stay inside these ranges and needn't reach their ends.
Inputs may be any that keep to these rules, and one draw needn't show every extreme that they name: `tile_lists`: entries beyond a tile's count are arbitrary ranks. The live entries of a tile are rising depth ranks of blocks owned by devices in the tile's own row of ty (block b belongs to device b // 96 of ty+tx, ty slowest). At most 3 live entries of one tile name blocks of one owner; in every row some owner is named 3 times by every tile of the row. No block is live in two entries. `tile_counts`: some tile has 24 in every draw. A permutation: depth_order[r] is the block at depth rank r. `gaussians`: row 2 (Z) lies between 1.5 and 12, row 6 (the quaternion's w) between 0.5 and 1.5.
All inputs are finite; a program needn't handle non-finite values.
Results may differ from the reference program's by a relative error of at most 0.0003.
Values sent between devices are 32-bit elements; how exact they have to be, the bound alone decides.
A program may use at most 64 MiB of HBM per device.

```python
import math
import jax
import jax.numpy as jnp
from jax import lax

TILE = 32
BLOCK = 128
FIELDS = 59
GROUP = 4
LMAX = 24
CAP = 3
BPD = 96
NB = 12288
HEIGHT = 256
WIDTH = 512
N_TY = 8
N_TX = 16


FOCAL = 1000.0


def owner_order(key):
    return jax.random.permutation(key, N_TX - 1)


def layout(key):
    keys = jax.random.split(jax.random.fold_in(key, 31), 8)
    devices = N_TY * N_TX
    depth_order = jax.random.permutation(keys[0], NB).astype(jnp.int32)
    rank_of = jnp.zeros((NB,), jnp.int32).at[depth_order].set(jnp.arange(NB, dtype=jnp.int32))
    special = jax.random.randint(keys[1], (N_TY,), 0, N_TX)
    tails = jax.vmap(owner_order)(jax.random.split(keys[2], devices)).astype(jnp.int32) + 1
    order = jnp.concatenate([jnp.zeros((devices, 1), jnp.int32), tails], axis=1)
    triples = LMAX // CAP
    row_of = jnp.arange(devices, dtype=jnp.int32) // N_TX
    col_of = jnp.arange(devices, dtype=jnp.int32) % N_TX
    owner_col = (special[row_of][:, None] + order[:, :triples]) % N_TX
    owner = row_of[:, None] * N_TX + owner_col
    shift = jax.random.randint(keys[3], (devices,), 0, N_TX)
    base = CAP * ((col_of[:, None] + shift[owner]) % N_TX)
    local = base[:, :, None] + jnp.arange(CAP, dtype=jnp.int32)[None, None, :]
    blocks = (owner[:, :, None] * BPD + local).reshape(devices, LMAX)
    short = jax.random.randint(keys[5], (devices,), 0, LMAX // 3 + 1)
    counts = jnp.maximum(CAP, LMAX - short)
    busy = jax.random.randint(keys[6], (), 0, devices)
    counts = jnp.where(jnp.arange(devices) == busy, LMAX, counts).astype(jnp.int32)
    slot = jnp.arange(LMAX, dtype=jnp.int32)
    live = slot[None, :] < counts[:, None]
    keyed = jnp.where(live, rank_of[blocks], NB + slot[None, :])
    ordered = jnp.sort(keyed, axis=1)
    filler = jax.random.randint(keys[7], (devices, LMAX), 0, NB)
    lists = jnp.where(live, ordered, filler).astype(jnp.int32)
    live_blocks = jnp.where(live, blocks, NB).reshape(-1)
    home = jnp.full((NB,), -1, jnp.int32).at[live_blocks].set(jnp.repeat(jnp.arange(devices, dtype=jnp.int32), LMAX), mode='drop')
    return (lists.reshape(N_TY, N_TX, LMAX), counts.reshape(N_TY, N_TX), depth_order, home)


def draw_tile_lists(key, part):
    return layout(key)[0]


def draw_tile_counts(key, part):
    return layout(key)[1]


def draw_depth_order(key, part):
    return layout(key)[2]


def draw_gaussians(key, part):
    home = layout(key)[3]
    keys = jax.random.split(jax.random.fold_in(key, 57), 12)
    shape = (NB, BLOCK)
    reach, small, large, dimmest, brightest, tint = (0.6, 1.0, 6.0, -4.0, -1.0, 1.0)
    width = float(TILE * N_TX)
    height = float(TILE * N_TY)
    placed = (home >= 0)[:, None]
    tile_col = (jnp.maximum(home, 0) % N_TX).astype(jnp.float32)[:, None]
    tile_row = (jnp.maximum(home, 0) // N_TX).astype(jnp.float32)[:, None]
    near_u = (tile_col + 0.5) * TILE + jax.random.uniform(keys[0], shape, minval=-reach, maxval=reach) * TILE
    near_v = (tile_row + 0.5) * TILE + jax.random.uniform(keys[1], shape, minval=-reach, maxval=reach) * TILE
    pos_u = jnp.where(placed, near_u, jax.random.uniform(keys[2], shape, minval=0.0, maxval=width))
    pos_v = jnp.where(placed, near_v, jax.random.uniform(keys[3], shape, minval=0.0, maxval=height))
    depth = jnp.exp(jax.random.uniform(keys[4], shape, minval=math.log(1.5), maxval=math.log(12.0)))
    mean_x = (pos_u - 0.5 * width) * depth / FOCAL
    mean_y = (pos_v - 0.5 * height) * depth / FOCAL
    pixel_sigma = jnp.exp(jax.random.uniform(keys[5], (3,) + shape, minval=math.log(small), maxval=math.log(large)))
    log_scale = jnp.log(pixel_sigma * depth[None] / FOCAL)
    quat_real = jax.random.uniform(keys[6], shape, minval=0.5, maxval=1.5)
    quat_imag = jax.random.uniform(keys[7], (3,) + shape, minval=-0.7, maxval=0.7)
    logit = jax.random.uniform(keys[8], shape, minval=dimmest, maxval=brightest)
    base_color = jax.random.uniform(keys[9], (3,) + shape, minval=-tint, maxval=tint)
    detail = jax.random.uniform(keys[10], (45,) + shape, minval=-0.3, maxval=0.3)
    rows = jnp.concatenate([jnp.stack([mean_x, mean_y, depth]), log_scale, quat_real[None], quat_imag, logit[None], base_color, detail], axis=0)
    return jnp.transpose(rows, (1, 0, 2)).astype(jnp.float32)


def block_scale(stream_key, extent, pieces, least, largest):
    level, own = 1.0, jax.random.fold_in(stream_key, 6)
    for dim, blocks in pieces:
        draws = jnp.exp(jax.random.uniform(jax.random.fold_in(own, dim), (blocks,), jnp.float32, least / len(pieces), largest / len(pieces)))
        level = level * jnp.repeat(draws, extent[dim] // blocks).reshape([-1 if axis == dim else 1 for axis in range(len(extent))])
    return level


def setup_inputs(seed: int = 0) -> dict:
    streams_of = jax.random.split(jax.random.key(seed), 6)
    gaussians = draw_gaussians(jax.random.fold_in(streams_of[5], 71), 0)
    tile_lists = draw_tile_lists(jax.random.fold_in(streams_of[5], 71), 0)
    tile_counts = draw_tile_counts(jax.random.fold_in(streams_of[5], 71), 0)
    depth_order = draw_depth_order(jax.random.fold_in(streams_of[5], 71), 0)
    target = jnp.clip(1.0 * jax.random.uniform(streams_of[4], (3, HEIGHT, WIDTH), jnp.float32) ** block_scale(streams_of[4], (3, HEIGHT, WIDTH), ((1, 8), (2, 16)), -0.2, 0.2), 0.0, 1.0)
    return {"gaussians": gaussians, "tile_lists": tile_lists, "tile_counts": tile_counts, "depth_order": depth_order, "target": target}


FOCAL = 1000.0
LOW_PASS = 0.3
STRUCT_WEIGHT = 0.2
LUMA_TERM = 0.0001
CONTRAST_TERM = 0.0009
ROBUST_TERM = 1e-06
HARMONIC_ZERO = 0.28209479177387814
HARMONIC_ONE = 0.4886025119029199
HARMONIC_TWO = (1.0925484305920792, -1.0925484305920792, 0.31539156525252005, -1.0925484305920792, 0.5462742152960396)
HARMONIC_THREE = (-0.5900435899266435, 2.890611442640554, -0.4570457994644658, 0.3731763325901154, -0.4570457994644658, 1.445305721320277, -0.5900435899266435)

def harmonics(dir_x, dir_y, dir_z):
    square_x = dir_x * dir_x
    square_y = dir_y * dir_y
    square_z = dir_z * dir_z
    pair_xy = dir_x * dir_y
    pair_yz = dir_y * dir_z
    pair_xz = dir_x * dir_z
    return jnp.stack([HARMONIC_ZERO * jnp.ones_like(dir_x), -HARMONIC_ONE * dir_y, HARMONIC_ONE * dir_z, -HARMONIC_ONE * dir_x, HARMONIC_TWO[0] * pair_xy, HARMONIC_TWO[1] * pair_yz, HARMONIC_TWO[2] * (2.0 * square_z - square_x - square_y), HARMONIC_TWO[3] * pair_xz, HARMONIC_TWO[4] * (square_x - square_y), HARMONIC_THREE[0] * dir_y * (3.0 * square_x - square_y), HARMONIC_THREE[1] * pair_xy * dir_z, HARMONIC_THREE[2] * dir_y * (4.0 * square_z - square_x - square_y), HARMONIC_THREE[3] * dir_z * (2.0 * square_z - 3.0 * square_x - 3.0 * square_y), HARMONIC_THREE[4] * dir_x * (4.0 * square_z - square_x - square_y), HARMONIC_THREE[5] * dir_z * (square_x - square_y), HARMONIC_THREE[6] * dir_x * (square_x - 3.0 * square_y)], axis=1)

def project(raw, center_x, center_y):
    count_rows = raw.shape[0]
    block = raw.shape[2]
    mean_x, mean_y, mean_z = (raw[:, 0], raw[:, 1], raw[:, 2])
    scale = jnp.exp(raw[:, 3:6])
    quat = raw[:, 6:10] / jnp.sqrt(lax.optimization_barrier(jnp.sum(raw[:, 6:10] * raw[:, 6:10], axis=1, keepdims=True)))
    real, imag_i, imag_j, imag_k = (quat[:, 0], quat[:, 1], quat[:, 2], quat[:, 3])
    rotation = [[1.0 - 2.0 * (imag_j * imag_j + imag_k * imag_k), 2.0 * (imag_i * imag_j - real * imag_k), 2.0 * (imag_i * imag_k + real * imag_j)], [2.0 * (imag_i * imag_j + real * imag_k), 1.0 - 2.0 * (imag_i * imag_i + imag_k * imag_k), 2.0 * (imag_j * imag_k - real * imag_i)], [2.0 * (imag_i * imag_k - real * imag_j), 2.0 * (imag_j * imag_k + real * imag_i), 1.0 - 2.0 * (imag_i * imag_i + imag_j * imag_j)]]
    scaled = [[rotation[row][col] * scale[:, col] for col in range(3)] for row in range(3)]
    sigma = [[sum((scaled[row][col] * scaled[other][col] for col in range(3))) for other in range(3)] for row in range(3)]
    inverse_z = 1.0 / mean_z
    jac_diag = FOCAL * inverse_z
    jac_xz = -FOCAL * mean_x * inverse_z * inverse_z
    jac_yz = -FOCAL * mean_y * inverse_z * inverse_z
    row_u = [jac_diag * sigma[0][col] + jac_xz * sigma[2][col] for col in range(3)]
    row_v = [jac_diag * sigma[1][col] + jac_yz * sigma[2][col] for col in range(3)]
    cov_uu = row_u[0] * jac_diag + row_u[2] * jac_xz + LOW_PASS
    cov_uv = row_u[1] * jac_diag + row_u[2] * jac_yz
    cov_vv = row_v[1] * jac_diag + row_v[2] * jac_yz + LOW_PASS
    determinant = cov_uu * cov_vv - cov_uv * cov_uv
    pos_u = FOCAL * mean_x * inverse_z + center_x
    pos_v = FOCAL * mean_y * inverse_z + center_y
    opacity = 0.99 * jax.nn.sigmoid(raw[:, 10])
    length = jnp.sqrt(mean_x * mean_x + mean_y * mean_y + mean_z * mean_z)
    basis = harmonics(mean_x / length, mean_y / length, mean_z / length)
    coeffs = raw[:, 11:59].reshape(count_rows, 16, 3, block)
    color = 0.5 + lax.optimization_barrier(jnp.sum(coeffs * basis[:, :, None, :], axis=1))
    shape_rows = jnp.stack([pos_u, pos_v, cov_vv / determinant, -cov_uv / determinant, cov_uu / determinant, opacity], axis=1)
    return jnp.concatenate([shape_rows, color], axis=1)

def composite(flat, live, pixel_x, pixel_y):
    delta_x = pixel_x[None, :] - flat[0][:, None]
    delta_y = pixel_y[None, :] - flat[1][:, None]
    power = flat[2][:, None] * delta_x * delta_x + 2.0 * flat[3][:, None] * delta_x * delta_y + flat[4][:, None] * delta_y * delta_y
    alpha = (live * flat[5])[:, None] * jnp.exp(-0.5 * power)
    keep = jnp.log1p(-alpha)
    before = jnp.cumsum(keep, axis=0) - keep
    weight = alpha * jnp.exp(before)
    color = jnp.dot(flat[6:9], weight, precision=lax.Precision.HIGHEST, preferred_element_type=jnp.float32)
    return (color, lax.optimization_barrier(jnp.sum(keep, axis=0)))

def to_groups(slot_flat, live):
    lmax, fields, block = slot_flat.shape
    steps_total = lmax // GROUP
    groups = slot_flat.reshape(steps_total, GROUP, fields, block).transpose(0, 2, 1, 3).reshape(steps_total, fields, GROUP * block)
    live_groups = jnp.repeat(live.astype(slot_flat.dtype), block).reshape(steps_total, GROUP * block)
    return (groups, live_groups)

def from_groups(grads, block):
    steps_total, fields, spread = grads.shape
    return grads.reshape(steps_total, fields, GROUP, block).transpose(0, 2, 1, 3).reshape(steps_total * GROUP, fields, block)

def render_forward(groups, live_groups, used, pixel_x, pixel_y):
    pixels = pixel_x.shape[0]

    def advance(index, carry):
        color, log_light, store = carry
        group_color, log_keep = composite(groups[index], live_groups[index], pixel_x, pixel_y)
        store = store.at[index].set(log_light)
        return (color + jnp.exp(log_light)[None, :] * group_color, log_light + log_keep, store)
    start = (jnp.zeros((3, pixels), jnp.float32), jnp.zeros((pixels,), jnp.float32), jnp.zeros((groups.shape[0], pixels), jnp.float32))
    color, final_light, store = lax.fori_loop(0, used, advance, start)
    return (color, store)

def render_backward(groups, live_groups, used, store, pixel_x, pixel_y, color_grad):

    def retreat(step, carry):
        behind, grads = carry
        index = used - 1 - step
        live_now = live_groups[index]

        def shade(flat):
            return composite(flat, live_now, pixel_x, pixel_y)
        (group_color, log_keep), pull = jax.vjp(shade, groups[index])
        light = jnp.exp(store[index])
        passed = light * jnp.exp(log_keep)
        flat_grad = pull((light[None, :] * color_grad, passed * lax.optimization_barrier(jnp.sum(color_grad * behind, axis=0))))[0]
        behind = group_color + jnp.exp(log_keep)[None, :] * behind
        return (behind, grads.at[index].set(flat_grad))
    start = (jnp.zeros_like(color_grad), jnp.zeros_like(groups))
    return lax.fori_loop(0, used, retreat, start)[1]

def window_taps():
    offsets = jnp.arange(11, dtype=jnp.float32) - 5.0
    taps = jnp.exp(-offsets * offsets / 4.5)
    return taps / jnp.sum(taps)

def filtered(field, taps):
    rows = field.shape[-2] - 10
    cols = field.shape[-1] - 10
    sideways = sum((taps[shift] * field[..., :, shift:shift + cols] for shift in range(11)))
    return sum((taps[shift] * sideways[..., shift:shift + rows, :] for shift in range(11)))

def similarity(mean_a, mean_b, square_a, square_b, cross):
    var_a = square_a - mean_a * mean_a
    var_b = square_b - mean_b * mean_b
    covar = cross - mean_a * mean_b
    top = (2.0 * mean_a * mean_b + LUMA_TERM) * (2.0 * covar + CONTRAST_TERM)
    bottom = (mean_a * mean_a + mean_b * mean_b + LUMA_TERM) * (var_a + var_b + CONTRAST_TERM)
    return top / bottom

def objective(image, target):
    taps = window_taps()

    def padded(field):
        return jnp.pad(field, ((0, 0), (5, 5), (5, 5)))
    score = similarity(filtered(padded(image), taps), filtered(padded(target), taps), filtered(padded(image * image), taps), filtered(padded(target * target), taps), filtered(padded(image * target), taps))
    gap = image - target
    robust = jnp.sqrt(gap * gap + ROBUST_TERM)
    return jnp.sum((1.0 - STRUCT_WEIGHT) * robust + STRUCT_WEIGHT * (1.0 - score))

def reference(gaussians, tile_lists, tile_counts, depth_order, target):
    height = TILE * N_TY
    width = TILE * N_TX
    center_x = 0.5 * width
    center_y = 0.5 * height

    def projector(raw):
        return project(raw, center_x, center_y)

    def tile_inputs(index):
        tile_row = index // N_TX
        tile_col = index % N_TX
        ranks = tile_lists[tile_row, tile_col]
        count = tile_counts[tile_row, tile_col]
        blocks = depth_order[ranks]
        raw = gaussians[blocks]
        live = jnp.arange(LMAX, dtype=jnp.int32) < count
        offsets = jnp.arange(TILE * TILE, dtype=jnp.int32)
        pixel_x = (tile_col * TILE + offsets % TILE).astype(jnp.float32) + 0.5
        pixel_y = (tile_row * TILE + offsets // TILE).astype(jnp.float32) + 0.5
        used = (count + GROUP - 1) // GROUP
        return (blocks, raw, live, pixel_x, pixel_y, used)

    def forward_tile(index):
        blocks, raw, live, pixel_x, pixel_y, used = tile_inputs(index)
        groups, live_groups = to_groups(projector(raw), live)
        return render_forward(groups, live_groups, used, pixel_x, pixel_y)
    tiles = jnp.arange(N_TY * N_TX, dtype=jnp.int32)
    colors, stores = lax.map(forward_tile, tiles)
    image = colors.reshape(N_TY, N_TX, 3, TILE, TILE).transpose(2, 0, 3, 1, 4).reshape(3, height, width)

    def scored(picture):
        return objective(picture, target)
    total, pull_total = jax.vjp(scored, image)
    image_grad = pull_total(jnp.ones_like(total))[0]
    tile_grads = image_grad.reshape(3, N_TY, TILE, N_TX, TILE).transpose(1, 3, 0, 2, 4).reshape(N_TY * N_TX, 3, TILE * TILE)

    def backward_tile(inputs):
        index, store, color_grad = inputs
        blocks, raw, live, pixel_x, pixel_y, used = tile_inputs(index)
        slot_flat, pull_raw = jax.vjp(projector, raw)
        groups, live_groups = to_groups(slot_flat, live)
        flat_grads = render_backward(groups, live_groups, used, store, pixel_x, pixel_y, color_grad)
        raw_grads = pull_raw(from_groups(flat_grads, BLOCK))[0]
        return (raw_grads * live.astype(raw_grads.dtype)[:, None, None], blocks)
    raw_grads, blocks = lax.map(backward_tile, (tiles, stores, tile_grads))
    gaussian_grads = jnp.zeros_like(gaussians).at[blocks.reshape(-1)].add(raw_grads.reshape(-1, FIELDS, BLOCK))
    return (gaussian_grads, total / (3.0 * height * width))
```

```python
import functools
import math

import jax
import jax.numpy as jnp
import numpy as np
from jax import lax
from jax.experimental import pallas as pl
from jax.experimental.pallas import tpu as pltpu
from jax.sharding import PartitionSpec as P

CAP = 3
SLOT = 8
LMAX = 24
BLOCK = 128
SIDE = 32
PIX = SIDE * SIDE
UNIT = 8
UNITS = LMAX // UNIT
ROWS = UNIT * BLOCK
CHUNK = 128
CHUNKS = ROWS // CHUNK
STEPS = CHUNK // UNIT
FIELDS = 59
WIDE = 9 * BLOCK

FOCAL = 1000.0
LOW_PASS = 0.3
STRUCT_WEIGHT = 0.2
LUMA_TERM = 0.0001
CONTRAST_TERM = 0.0009
ROBUST_TERM = 1e-06
LOG2E = math.log2(math.e)
HARMONIC_ZERO = 0.28209479177387814
HARMONIC_ONE = 0.4886025119029199
HARMONIC_TWO = (
    1.0925484305920792,
    -1.0925484305920792,
    0.31539156525252005,
    -1.0925484305920792,
    0.5462742152960396,
)
HARMONIC_THREE = (
    -0.5900435899266435,
    2.890611442640554,
    -0.4570457994644658,
    0.3731763325901154,
    -0.4570457994644658,
    1.445305721320277,
    -0.5900435899266435,
)
VMEM = pltpu.VMEM
F32 = jnp.float32
BF16 = jnp.bfloat16


def harmonics(dir_x, dir_y, dir_z):
    square_x = dir_x * dir_x
    square_y = dir_y * dir_y
    square_z = dir_z * dir_z
    pair_xy = dir_x * dir_y
    pair_yz = dir_y * dir_z
    pair_xz = dir_x * dir_z
    return [
        HARMONIC_ZERO * jnp.ones_like(dir_x),
        -HARMONIC_ONE * dir_y,
        HARMONIC_ONE * dir_z,
        -HARMONIC_ONE * dir_x,
        HARMONIC_TWO[0] * pair_xy,
        HARMONIC_TWO[1] * pair_yz,
        HARMONIC_TWO[2] * (2.0 * square_z - square_x - square_y),
        HARMONIC_TWO[3] * pair_xz,
        HARMONIC_TWO[4] * (square_x - square_y),
        HARMONIC_THREE[0] * dir_y * (3.0 * square_x - square_y),
        HARMONIC_THREE[1] * pair_xy * dir_z,
        HARMONIC_THREE[2] * dir_y * (4.0 * square_z - square_x - square_y),
        HARMONIC_THREE[3] * dir_z * (2.0 * square_z - 3.0 * square_x - 3.0 * square_y),
        HARMONIC_THREE[4] * dir_x * (4.0 * square_z - square_x - square_y),
        HARMONIC_THREE[5] * dir_z * (square_x - square_y),
        HARMONIC_THREE[6] * dir_x * (square_x - 3.0 * square_y),
    ]


def shape_of(center_x, center_y, mean_x, mean_y, mean_z, s0, s1, s2, q0, q1, q2, q3, logit):
    scale = [jnp.exp(s0), jnp.exp(s1), jnp.exp(s2)]
    norm = 1.0 / jnp.sqrt(q0 * q0 + q1 * q1 + q2 * q2 + q3 * q3)
    real, imag_i, imag_j, imag_k = q0 * norm, q1 * norm, q2 * norm, q3 * norm
    rotation = [
        [
            1.0 - 2.0 * (imag_j * imag_j + imag_k * imag_k),
            2.0 * (imag_i * imag_j - real * imag_k),
            2.0 * (imag_i * imag_k + real * imag_j),
        ],
        [
            2.0 * (imag_i * imag_j + real * imag_k),
            1.0 - 2.0 * (imag_i * imag_i + imag_k * imag_k),
            2.0 * (imag_j * imag_k - real * imag_i),
        ],
        [
            2.0 * (imag_i * imag_k - real * imag_j),
            2.0 * (imag_j * imag_k + real * imag_i),
            1.0 - 2.0 * (imag_i * imag_i + imag_j * imag_j),
        ],
    ]
    scaled = [[rotation[row][col] * scale[col] for col in range(3)] for row in range(3)]

    def sigma(row, other):
        a, b = scaled[row], scaled[other]
        return a[0] * b[0] + a[1] * b[1] + a[2] * b[2]

    xx, xy, xz = sigma(0, 0), sigma(0, 1), sigma(0, 2)
    yy, yz, zz = sigma(1, 1), sigma(1, 2), sigma(2, 2)
    inverse_z = 1.0 / mean_z
    diag = FOCAL * inverse_z
    jac_xz = -FOCAL * mean_x * inverse_z * inverse_z
    jac_yz = -FOCAL * mean_y * inverse_z * inverse_z
    u0, u1, u2 = diag * xx + jac_xz * xz, diag * xy + jac_xz * yz, diag * xz + jac_xz * zz
    v1, v2 = diag * yy + jac_yz * yz, diag * yz + jac_yz * zz
    cov_uu = u0 * diag + u2 * jac_xz + LOW_PASS
    cov_uv = u1 * diag + u2 * jac_yz
    cov_vv = v1 * diag + v2 * jac_yz + LOW_PASS
    inverse = 1.0 / (cov_uu * cov_vv - cov_uv * cov_uv)
    pos_u = FOCAL * mean_x * inverse_z + center_x
    pos_v = FOCAL * mean_y * inverse_z + center_y
    log_opacity = jnp.log(0.99 / (1.0 + jnp.exp(-logit)))
    return pos_u, pos_v, cov_vv * inverse, -cov_uv * inverse, cov_uu * inverse, log_opacity


def basis_of(mean_x, mean_y, mean_z):
    inverse = 1.0 / jnp.sqrt(mean_x * mean_x + mean_y * mean_y + mean_z * mean_z)
    return harmonics(mean_x * inverse, mean_y * inverse, mean_z * inverse)


def pieces(x, count):
    out = []
    for left in range(count):
        part = x.astype(BF16).astype(F32)
        out.append(part)
        if left < count - 1:
            x = x - part
    return out


def project_kernel(owned, center, ranks, count, order, place, g_ref, out_ref, req_ref, slot_ref, used):
    step = pl.program_id(0)

    @pl.when(step == 0)
    def _():
        req_ref[...] = jnp.full_like(req_ref, -1)
        first = place[0]
        for o in range(req_ref.shape[0] // SLOT):
            used[o] = 0

        def put(k, carry):
            block = order[ranks[k]]
            home = block // owned
            owner = home - first
            local = block - home * owned

            @pl.when(k < count[0])
            def _():
                row = owner * SLOT + used[owner]
                used[owner] = used[owner] + 1
                slot_ref[k] = row
                req_ref[pl.ds(row, 1), :] = jnp.full((1, BLOCK), local, jnp.int32)

            @pl.when(k >= count[0])
            def _():
                slot_ref[k] = SLOT - 1

            return carry

        lax.fori_loop(0, LMAX, put, 0)

    field = [g_ref[:, f, :] for f in range(11)]
    shape = shape_of(center[0], center[1], *field)
    basis = basis_of(*field[:3])
    for f in range(6):
        out_ref[:, f * BLOCK : (f + 1) * BLOCK] = shape[f]
    for ch in range(3):
        color = jnp.full((UNIT, BLOCK), 0.5, F32)
        for m in range(16):
            color = color + g_ref[:, 11 + 3 * m + ch, :] * basis[m]
        out_ref[:, (6 + ch) * BLOCK : (7 + ch) * BLOCK] = color


def project_blocks(gaussians, ranks, count, order, place, center, peers):
    owned = gaussians.shape[0]
    smem = pl.BlockSpec(memory_space=pltpu.SMEM)
    return pl.pallas_call(
        functools.partial(project_kernel, owned, center),
        grid=(owned // UNIT,),
        in_specs=[smem, smem, smem, smem, pl.BlockSpec((UNIT, FIELDS, BLOCK), lambda i: (i, 0, 0))],
        out_specs=[
            pl.BlockSpec((UNIT, WIDE), lambda i: (i, 0)),
            pl.BlockSpec((peers * SLOT, BLOCK), lambda i: (0, 0)),
            smem,
        ],
        out_shape=[
            jax.ShapeDtypeStruct((owned, WIDE), F32),
            jax.ShapeDtypeStruct((peers * SLOT, BLOCK), jnp.int32),
            jax.ShapeDtypeStruct((LMAX,), jnp.int32),
        ],
        scratch_shapes=[pltpu.SMEM((peers,), jnp.int32)],
        name="project",
    )(ranks, count, order, place, gaussians)


def features():
    offset = np.arange(PIX)
    x = (offset % SIDE - SIDE // 2).astype(np.float32)
    y = (offset // SIDE - SIDE // 2).astype(np.float32)
    six = np.stack([np.ones_like(x), x, y, x * x, x * y, y * y])
    ahead = np.zeros((32, PIX), np.float32)
    for piece in range(3):
        ahead[6 * piece : 6 * piece + 6] = six
    back = np.zeros((16, PIX), np.float32)
    back[:6] = six
    return jnp.asarray(ahead, BF16), jnp.asarray(back, BF16)


def load_entries(slot_ref, recv_ref, ent_ref):
    for k in range(LMAX):
        ent_ref[k : k + 1, :] = recv_ref[pl.ds(slot_ref[k], 1), :]


def build_rows(place, count, ent_ref, field_ref, row_ref):
    mid_x = place[2].astype(F32)
    mid_y = place[1].astype(F32)
    mid_x = mid_x * SIDE + (SIDE // 2 + 0.5)
    mid_y = mid_y * SIDE + (SIDE // 2 + 0.5)
    field_ref[...] = jnp.zeros_like(field_ref)
    for unit in range(UNITS):
        rows = slice(unit * UNIT, (unit + 1) * UNIT)
        u, v, a, b, c, log_o, r0, r1, r2 = [
            ent_ref[rows, f * BLOCK : (f + 1) * BLOCK] for f in range(9)
        ]
        entry = lax.broadcasted_iota(jnp.int32, (UNIT, BLOCK), 0) + unit * UNIT
        live = entry < count[0]
        du, dv = u - mid_x, v - mid_y
        k = -0.5 * LOG2E
        mix_u, mix_v = a * du + b * dv, b * du + c * dv
        coefs = [
            jnp.where(live, k * (mix_u * du + mix_v * dv) + LOG2E * log_o, -1e4),
            -2.0 * k * mix_u,
            -2.0 * k * mix_v,
            k * a,
            2.0 * k * b,
            k * c,
        ]
        coefs = coefs[:1] + [jnp.where(live, q, 0.0) for q in coefs[1:]]
        color = [jnp.where(live, r, 0.0) for r in (r0, r1, r2)]
        split = [pieces(q, 3) for q in coefs]
        shade = [pieces(r, 2) for r in color]
        columns = [split[f][piece] for piece in range(3) for f in range(6)]
        columns += [s[0] for s in shade] + [s[0] for s in shade] + [s[1] for s in shade]
        columns += color
        for f, column in enumerate(columns):
            field_ref[f * UNIT : (f + 1) * UNIT, :] = column
        for s in range(UNIT):
            table = field_ref[pl.ds(s, 32, stride=UNIT), :].T
            table = jnp.concatenate([table, jnp.zeros((BLOCK, BLOCK - 32), F32)], axis=1)
            row_ref[pl.ds(unit * ROWS + s, BLOCK, stride=UNIT), :] = table


def exponent_chunk(row_ref, ahead, chunk, alpha_ref):
    base = pl.multiple_of(chunk * CHUNK, CHUNK)
    rows = row_ref[pl.ds(base, CHUNK), :][:, :32].astype(BF16)
    alpha_ref[...] = jnp.exp2(jnp.dot(rows, ahead, preferred_element_type=F32))


def scan_chunk(row_ref, chunk, alpha_ref, carry):
    light, c0, c1, c2 = carry
    base = pl.multiple_of(chunk * CHUNK, CHUNK)
    for i in range(STEPS):
        alpha = alpha_ref[i * UNIT : (i + 1) * UNIT, :]
        shade = row_ref[pl.ds(base + i * UNIT, UNIT), :]
        weight = alpha * light
        light = light - weight
        c0 = c0 + shade[:, 27:28] * weight
        c1 = c1 + shade[:, 28:29] * weight
        c2 = c2 + shade[:, 29:30] * weight
    return light, c0, c1, c2


def forward_kernel(slot_ref, count, place, ahead_ref, recv_ref, image_ref, light_ref, color_ref,
                   row_ref, ent_ref, field_ref, even_ref, odd_ref):
    load_entries(slot_ref, recv_ref, ent_ref)
    build_rows(place, count, ent_ref, field_ref, row_ref)
    ahead = ahead_ref[...]
    last = UNITS * CHUNKS - 1
    exponent_chunk(row_ref, ahead, 0, even_ref)
    for unit in range(UNITS):
        zero = jnp.zeros((UNIT, PIX), F32)

        def advance(step, carry):
            chunk = unit * CHUNKS + 2 * step
            exponent_chunk(row_ref, ahead, chunk + 1, odd_ref)
            carry = scan_chunk(row_ref, chunk, even_ref, carry)
            exponent_chunk(row_ref, ahead, jnp.minimum(chunk + 2, last), even_ref)
            return scan_chunk(row_ref, chunk + 1, odd_ref, carry)

        light, c0, c1, c2 = lax.fori_loop(0, CHUNKS // 2, advance, (zero + 1.0, zero, zero, zero))
        rows = slice(unit * UNIT, (unit + 1) * UNIT)
        light_ref[rows, :] = light
        color_ref[0, rows, :] = c0
        color_ref[1, rows, :] = c1
        color_ref[2, rows, :] = c2
    light = jnp.ones((1, PIX), F32)
    image = [jnp.zeros((1, PIX), F32) for _ in range(3)]
    for k in range(LMAX):
        for ch in range(3):
            image[ch] = image[ch] + light * color_ref[ch, k : k + 1, :]
        light = light * light_ref[k : k + 1, :]
    for ch in range(3):
        for j in range(8):
            image_ref[ch, j : j + 1, :] = image[ch][:, j * BLOCK : (j + 1) * BLOCK]


def render(slots, count, place, ahead, recv):
    smem = pl.BlockSpec(memory_space=pltpu.SMEM)
    vmem = pl.BlockSpec(memory_space=pltpu.VMEM)
    return pl.pallas_call(
        forward_kernel,
        in_specs=[smem, smem, smem, vmem, vmem],
        out_specs=[vmem, vmem, vmem],
        out_shape=[
            jax.ShapeDtypeStruct((3, 8, BLOCK), F32),
            jax.ShapeDtypeStruct((LMAX, PIX), F32),
            jax.ShapeDtypeStruct((3, LMAX, PIX), F32),
        ],
        scratch_shapes=[
            VMEM((UNITS * ROWS, BLOCK), F32),
            VMEM((LMAX, WIDE), F32),
            VMEM((32 * UNIT, BLOCK), F32),
            VMEM((CHUNK, PIX), F32),
            VMEM((CHUNK, PIX), F32),
        ],
        name="render",
    )(slots, count, place, ahead, recv)


def long_row(ref, ch):
    return jnp.concatenate([ref[ch, j : j + 1, :] for j in range(8)], axis=1)


NT = (((1,), (1,)), ((), ()))


def backward_kernel(slot_ref, count, place, ahead_ref, back_ref, recv_ref, light_ref, color_ref, grad_ref,
                    out_ref, row_ref, ent_ref, field_ref, alpha_ref, weight_ref, shade_ref, start_ref,
                    behind_ref, moment_ref, result_ref):
    load_entries(slot_ref, recv_ref, ent_ref)
    build_rows(place, count, ent_ref, field_ref, row_ref)
    ahead = ahead_ref[...]
    grad = [long_row(grad_ref, ch) for ch in range(3)]
    high = [g.astype(BF16).astype(F32) for g in grad]
    low = [g - h for g, h in zip(grad, high)]
    zero = [jnp.zeros((1, PIX), F32)]
    mixed = jnp.concatenate(zero * 18 + high + low + high + zero * 5, axis=0).astype(BF16)
    tail = jnp.concatenate(zero * 8 + high + low + zero * 2, axis=0).astype(BF16)
    back = back_ref[...]

    light = jnp.ones((1, PIX), F32)
    for k in range(LMAX):
        start_ref[k : k + 1, :] = light
        light = light * light_ref[k : k + 1, :]
    behind = jnp.zeros((1, PIX), F32)
    for k in reversed(range(LMAX)):
        behind_ref[k : k + 1, :] = behind
        own = sum(grad[ch] * color_ref[ch, k : k + 1, :] for ch in range(3))
        behind = own + light_ref[k : k + 1, :] * behind

    def unit_pass(unit, carry):
        rows = pl.ds(pl.multiple_of(unit * UNIT, UNIT), UNIT)

        def recompute(chunk, light):
            base = pl.multiple_of(chunk * CHUNK, CHUNK)
            total = pl.multiple_of(unit * ROWS + base, CHUNK)
            packed = row_ref[pl.ds(total, CHUNK), :][:, :32].astype(BF16)
            alpha_ref[pl.ds(base, CHUNK), :] = jnp.exp2(jnp.dot(packed, ahead, preferred_element_type=F32))
            for i in range(STEPS):
                weight = alpha_ref[pl.ds(base + i * UNIT, UNIT), :] * light
                light = light - weight
                weight_ref[pl.ds(base + i * UNIT, UNIT), :] = weight
            return light

        lax.fori_loop(0, CHUNKS, recompute, start_ref[rows, :])

        def retreat(step, behind):
            base = pl.multiple_of((CHUNKS - 1 - step) * CHUNK, CHUNK)
            total = pl.multiple_of(unit * ROWS + base, CHUNK)
            packed = row_ref[pl.ds(total, CHUNK), :][:, :32].astype(BF16)
            shade_ref[...] = jnp.dot(packed, mixed, preferred_element_type=F32)
            for i in reversed(range(STEPS)):
                here = slice(i * UNIT, (i + 1) * UNIT)
                gap = shade_ref[here, :] - behind
                behind = behind + alpha_ref[pl.ds(base + i * UNIT, UNIT), :] * gap
                shade_ref[here, :] = weight_ref[pl.ds(base + i * UNIT, UNIT), :] * gap
            slope = shade_ref[...]
            weight = weight_ref[pl.ds(base, CHUNK), :]
            slope_high = slope.astype(BF16)
            slope_low = (slope - slope_high.astype(F32)).astype(BF16)
            weight_high = weight.astype(BF16)
            weight_low = (weight - weight_high.astype(F32)).astype(BF16)
            moment = lax.dot_general(slope_high, back, NT, preferred_element_type=F32)
            moment += lax.dot_general(slope_low, back, NT, preferred_element_type=F32)
            moment += lax.dot_general(weight_high, tail, NT, preferred_element_type=F32)
            moment += lax.dot_general(weight_low, tail, NT, preferred_element_type=F32)
            moment_ref[pl.ds(total, CHUNK), 0:16] = moment
            return behind

        lax.fori_loop(0, CHUNKS, retreat, behind_ref[rows, :])
        return carry

    moment_ref[...] = jnp.zeros_like(moment_ref)
    lax.fori_loop(0, UNITS, unit_pass, 0)

    mid_x = place[2].astype(F32) * SIDE + (SIDE // 2 + 0.5)
    mid_y = place[1].astype(F32) * SIDE + (SIDE // 2 + 0.5)
    for unit in range(UNITS):
        rows = slice(unit * UNIT, (unit + 1) * UNIT)
        for s in range(UNIT):
            table = moment_ref[pl.ds(unit * ROWS + s, BLOCK, stride=UNIT), :].T
            field_ref[pl.ds(s, 16, stride=UNIT), :] = table[:16]
        m = [field_ref[f * UNIT : (f + 1) * UNIT, :] for f in range(14)]
        u, v, a, b, c = [ent_ref[rows, f * BLOCK : (f + 1) * BLOCK] for f in range(5)]
        du, dv = u - mid_x, v - mid_y
        near_x, near_y = m[1] - du * m[0], m[2] - dv * m[0]
        values = [
            a * near_x + b * near_y,
            b * near_x + c * near_y,
            -0.5 * (m[3] - du * (m[1] + near_x)),
            -(m[4] - du * m[2] - dv * near_x),
            -0.5 * (m[5] - dv * (m[2] + near_y)),
            m[0],
            m[8] + m[11],
            m[9] + m[12],
            m[10] + m[13],
        ]
        for f, value in enumerate(values):
            result_ref[rows, f * BLOCK : (f + 1) * BLOCK] = value
    for k in range(LMAX):
        out_ref[pl.ds(slot_ref[k], 1), :] = result_ref[k : k + 1, :]


def render_gradient(slots, count, place, ahead, back, recv, light, color, grad):
    smem = pl.BlockSpec(memory_space=pltpu.SMEM)
    vmem = pl.BlockSpec(memory_space=pltpu.VMEM)
    return pl.pallas_call(
        backward_kernel,
        in_specs=[smem, smem, smem] + [vmem] * 6,
        out_specs=vmem,
        out_shape=jax.ShapeDtypeStruct(recv.shape, F32),
        scratch_shapes=[
            VMEM((UNITS * ROWS, BLOCK), F32),
            VMEM((LMAX, WIDE), F32),
            VMEM((32 * UNIT, BLOCK), F32),
            VMEM((ROWS, PIX), F32),
            VMEM((ROWS, PIX), F32),
            VMEM((CHUNK, PIX), F32),
            VMEM((LMAX, PIX), F32),
            VMEM((LMAX, PIX), F32),
            VMEM((UNITS * ROWS, BLOCK), F32),
            VMEM((LMAX, WIDE), F32),
        ],
        name="render_gradient",
    )(slots, count, place, ahead, back, recv, light, color, grad)


def pull_kernel(center, req_ref, back_ref, g_ref, out_ref, dense_ref):
    step = pl.program_id(0)

    @pl.when(step == 0)
    def _():
        owned = dense_ref.shape[0]
        req = req_ref[...]
        lane = lax.broadcasted_iota(jnp.int32, req.shape, 1)
        chosen = jnp.where(req == lane, 1.0, 0.0).T[:owned].astype(BF16)
        asked = req >= 0
        for f in range(9):
            cols = slice(f * BLOCK, (f + 1) * BLOCK)
            value = jnp.where(asked, back_ref[:, cols], 0.0)
            dense_ref[:, cols] = sum(
                jnp.dot(chosen, part.astype(BF16), preferred_element_type=F32) for part in pieces(value, 3)
            )

    rows = pl.ds(pl.multiple_of(step * UNIT, UNIT), UNIT)
    cot = [dense_ref[rows, f * BLOCK : (f + 1) * BLOCK] for f in range(9)]
    field = [g_ref[:, f, :] for f in range(11)]
    _, pull = jax.vjp(functools.partial(shape_of, center[0], center[1]), *field)
    grads = list(pull(tuple(cot[:6])))
    basis, pull_basis = jax.vjp(basis_of, *field[:3])
    basis_cot = []
    for m in range(16):
        total = jnp.zeros((UNIT, BLOCK), F32)
        for ch in range(3):
            total = total + g_ref[:, 11 + 3 * m + ch, :] * cot[6 + ch]
            out_ref[:, 11 + 3 * m + ch, :] = basis[m] * cot[6 + ch]
        basis_cot.append(total)
    extra = pull_basis(basis_cot)
    for f in range(3):
        grads[f] = grads[f] + extra[f]
    for f in range(11):
        out_ref[:, f, :] = grads[f]


def pull_blocks(req, back, gaussians, center):
    owned = gaussians.shape[0]
    return pl.pallas_call(
        functools.partial(pull_kernel, center),
        grid=(owned // UNIT,),
        in_specs=[
            pl.BlockSpec(req.shape, lambda i: (0, 0)),
            pl.BlockSpec(back.shape, lambda i: (0, 0)),
            pl.BlockSpec((UNIT, FIELDS, BLOCK), lambda i: (i, 0, 0)),
        ],
        out_specs=pl.BlockSpec((UNIT, FIELDS, BLOCK), lambda i: (i, 0, 0)),
        out_shape=jax.ShapeDtypeStruct(gaussians.shape, F32),
        scratch_shapes=[VMEM((owned, WIDE), F32)],
        name="pull",
    )(req, back, gaussians)


def extended(x, sides, width):
    for axis, dim in sides:
        size, length = (lax.axis_size(axis), x.shape[dim])
        up = [(i, (i + 1) % size) for i in range(size - 1)]
        down = [(j, i) for i, j in up]
        last = lax.slice_in_dim(x, length - width, length, axis=dim)
        first = lax.slice_in_dim(x, 0, width, axis=dim)
        before = lax.ppermute(last, axis, up)
        after = lax.ppermute(first, axis, down)
        x = jnp.concatenate([before, x, after], axis=dim)
    return x


def window_taps():
    offsets = np.arange(11, dtype=np.float32) - 5.0
    taps = np.exp(-offsets * offsets / 4.5)
    return taps / np.sum(taps)


def filtered(field, taps):
    rows = field.shape[-2] - 10
    cols = field.shape[-1] - 10
    sideways = sum((taps[shift] * field[..., :, shift : shift + cols] for shift in range(11)))
    return sum((taps[shift] * sideways[..., shift : shift + rows, :] for shift in range(11)))


def similarity(mean_a, mean_b, square_a, square_b, cross):
    var_a = square_a - mean_a * mean_a
    var_b = square_b - mean_b * mean_b
    covar = cross - mean_a * mean_b
    top = (2.0 * mean_a * mean_b + LUMA_TERM) * (2.0 * covar + CONTRAST_TERM)
    bottom = (mean_a * mean_a + mean_b * mean_b + LUMA_TERM) * (var_a + var_b + CONTRAST_TERM)
    return top / bottom


def moments(picture, goal, taps):
    return (
        filtered(picture, taps),
        filtered(goal, taps),
        filtered(picture * picture, taps),
        filtered(goal * goal, taps),
        filtered(picture * goal, taps),
    )


def per_device(gaussians, tile_lists, tile_counts, depth_order, target):
    across = lax.axis_size("tx")
    row_index = lax.axis_index("ty")
    col_index = lax.axis_index("tx")
    height = SIDE * lax.axis_size("ty")
    width = SIDE * across
    center = (0.5 * width, 0.5 * height)
    ranks = tile_lists.reshape(LMAX)
    count = tile_counts.reshape(1)
    place = jnp.stack([row_index * across, row_index, col_index]).astype(jnp.int32)
    table, req, slots = project_blocks(gaussians, ranks, count, depth_order, place, center, across)
    asked = lax.all_to_all(req, "tx", split_axis=0, concat_axis=0, tiled=True)
    local = asked[:, 0]
    served = table[jnp.maximum(local, 0)]
    recv = lax.all_to_all(served, "tx", split_axis=0, concat_axis=0, tiled=True)
    ahead, back = features()
    flat_image, light, color = render(slots, count, place, ahead, recv)
    image = flat_image.reshape(3, SIDE, SIDE)
    taps = window_taps()
    stacked = jnp.stack([image, target])
    framed = extended(stacked, (("ty", 2), ("tx", 3)), 5)
    maps = moments(framed[0], framed[1], taps)
    score, pull_score = jax.vjp(similarity, *maps)
    parts = pull_score(jnp.full_like(score, -STRUCT_WEIGHT))
    coeffs = jnp.stack([parts[0], parts[2], parts[4]])
    spread = extended(coeffs, (("ty", 2), ("tx", 3)), 5)
    smoothed = filtered(spread, taps)
    gap = image - target
    robust = jnp.sqrt(gap * gap + ROBUST_TERM)
    local_total = jnp.sum((1.0 - STRUCT_WEIGHT) * robust + STRUCT_WEIGHT * (1.0 - score))
    image_grad = (
        smoothed[0]
        + 2.0 * image * smoothed[1]
        + target * smoothed[2]
        + (1.0 - STRUCT_WEIGHT) * gap / robust
    )
    total = lax.psum(local_total, ("ty", "tx"))
    grads = render_gradient(
        slots, count, place, ahead, back, recv, light, color, image_grad.reshape(3, 8, BLOCK)
    )
    returned = lax.all_to_all(grads, "tx", split_axis=0, concat_axis=0, tiled=True)
    return pull_blocks(asked, returned, gaussians, center), total / (3.0 * height * width)


def solution(mesh):
    return jax.shard_map(
        per_device,
        mesh=mesh,
        in_specs=(
            P(("ty", "tx"), None, None),
            P("ty", "tx", None),
            P("ty", "tx"),
            P(),
            P(None, "ty", "tx"),
        ),
        out_specs=(P(("ty", "tx"), None, None), P()),
        check_vma=False,
    )
```

```python
import functools
import math

import jax
import jax.numpy as jnp
import numpy as np
from jax import lax
from jax.experimental import pallas as pl
from jax.experimental.pallas import tpu as pltpu
from jax.sharding import PartitionSpec as P

CAP = 3
SLOT = 8
LMAX = 24
BLOCK = 128
SIDE = 32
PIX = SIDE * SIDE
UNIT = 8
UNITS = LMAX // UNIT
ROWS = UNIT * BLOCK
CHUNK = 128
CHUNKS = ROWS // CHUNK
STEPS = CHUNK // UNIT
FIELDS = 59
NUMBERS = 9
WIDE = NUMBERS * BLOCK
PACK = CAP * NUMBERS
PER_STEP = 24

FOCAL = 1000.0
LOW_PASS = 0.3
STRUCT_WEIGHT = 0.2
LUMA_TERM = 0.0001
CONTRAST_TERM = 0.0009
ROBUST_TERM = 1e-06
LOG2E = math.log2(math.e)
HARMONIC_ZERO = 0.28209479177387814
HARMONIC_ONE = 0.4886025119029199
HARMONIC_TWO = (
    1.0925484305920792,
    -1.0925484305920792,
    0.31539156525252005,
    -1.0925484305920792,
    0.5462742152960396,
)
HARMONIC_THREE = (
    -0.5900435899266435,
    2.890611442640554,
    -0.4570457994644658,
    0.3731763325901154,
    -0.4570457994644658,
    1.445305721320277,
    -0.5900435899266435,
)
VMEM = pltpu.VMEM
F32 = jnp.float32
BF16 = jnp.bfloat16


def harmonics(dir_x, dir_y, dir_z):
    square_x = dir_x * dir_x
    square_y = dir_y * dir_y
    square_z = dir_z * dir_z
    pair_xy = dir_x * dir_y
    pair_yz = dir_y * dir_z
    pair_xz = dir_x * dir_z
    return [
        HARMONIC_ZERO * jnp.ones_like(dir_x),
        -HARMONIC_ONE * dir_y,
        HARMONIC_ONE * dir_z,
        -HARMONIC_ONE * dir_x,
        HARMONIC_TWO[0] * pair_xy,
        HARMONIC_TWO[1] * pair_yz,
        HARMONIC_TWO[2] * (2.0 * square_z - square_x - square_y),
        HARMONIC_TWO[3] * pair_xz,
        HARMONIC_TWO[4] * (square_x - square_y),
        HARMONIC_THREE[0] * dir_y * (3.0 * square_x - square_y),
        HARMONIC_THREE[1] * pair_xy * dir_z,
        HARMONIC_THREE[2] * dir_y * (4.0 * square_z - square_x - square_y),
        HARMONIC_THREE[3] * dir_z * (2.0 * square_z - 3.0 * square_x - 3.0 * square_y),
        HARMONIC_THREE[4] * dir_x * (4.0 * square_z - square_x - square_y),
        HARMONIC_THREE[5] * dir_z * (square_x - square_y),
        HARMONIC_THREE[6] * dir_x * (square_x - 3.0 * square_y),
    ]


def shape_of(center_x, center_y, mean_x, mean_y, mean_z, s0, s1, s2, q0, q1, q2, q3, logit):
    scale = [jnp.exp(s0), jnp.exp(s1), jnp.exp(s2)]
    norm = 1.0 / jnp.sqrt(q0 * q0 + q1 * q1 + q2 * q2 + q3 * q3)
    real, imag_i, imag_j, imag_k = q0 * norm, q1 * norm, q2 * norm, q3 * norm
    rotation = [
        [
            1.0 - 2.0 * (imag_j * imag_j + imag_k * imag_k),
            2.0 * (imag_i * imag_j - real * imag_k),
            2.0 * (imag_i * imag_k + real * imag_j),
        ],
        [
            2.0 * (imag_i * imag_j + real * imag_k),
            1.0 - 2.0 * (imag_i * imag_i + imag_k * imag_k),
            2.0 * (imag_j * imag_k - real * imag_i),
        ],
        [
            2.0 * (imag_i * imag_k - real * imag_j),
            2.0 * (imag_j * imag_k + real * imag_i),
            1.0 - 2.0 * (imag_i * imag_i + imag_j * imag_j),
        ],
    ]
    scaled = [[rotation[row][col] * scale[col] for col in range(3)] for row in range(3)]

    def sigma(row, other):
        a, b = scaled[row], scaled[other]
        return a[0] * b[0] + a[1] * b[1] + a[2] * b[2]

    xx, xy, xz = sigma(0, 0), sigma(0, 1), sigma(0, 2)
    yy, yz, zz = sigma(1, 1), sigma(1, 2), sigma(2, 2)
    inverse_z = 1.0 / mean_z
    diag = FOCAL * inverse_z
    jac_xz = -FOCAL * mean_x * inverse_z * inverse_z
    jac_yz = -FOCAL * mean_y * inverse_z * inverse_z
    u0, u1, u2 = diag * xx + jac_xz * xz, diag * xy + jac_xz * yz, diag * xz + jac_xz * zz
    v1, v2 = diag * yy + jac_yz * yz, diag * yz + jac_yz * zz
    cov_uu = u0 * diag + u2 * jac_xz + LOW_PASS
    cov_uv = u1 * diag + u2 * jac_yz
    cov_vv = v1 * diag + v2 * jac_yz + LOW_PASS
    inverse = 1.0 / (cov_uu * cov_vv - cov_uv * cov_uv)
    pos_u = FOCAL * mean_x * inverse_z + center_x
    pos_v = FOCAL * mean_y * inverse_z + center_y
    log_opacity = jnp.log(0.99 / (1.0 + jnp.exp(-logit)))
    return pos_u, pos_v, cov_vv * inverse, -cov_uv * inverse, cov_uu * inverse, log_opacity


def basis_of(mean_x, mean_y, mean_z):
    inverse = 1.0 / jnp.sqrt(mean_x * mean_x + mean_y * mean_y + mean_z * mean_z)
    return harmonics(mean_x * inverse, mean_y * inverse, mean_z * inverse)


def pieces(x, count):
    out = []
    for left in range(count):
        part = x.astype(BF16).astype(F32)
        out.append(part)
        if left < count - 1:
            x = x - part
    return out


def project_kernel(owned, center, ranks, count, order, place, g_ref, out_ref, req_ref, slot_ref, used):
    step = pl.program_id(0)

    @pl.when(step == 0)
    def _():
        req_ref[...] = jnp.full_like(req_ref, -1)
        first = place[0]
        for o in range(req_ref.shape[0]):
            used[o] = 0

        def put(k, carry):
            block = order[ranks[k]]
            home = block // owned
            owner = home - first
            local = block - home * owned

            @pl.when(k < count[0])
            def _():
                turn = used[owner]
                used[owner] = turn + 1
                slot_ref[k] = owner * SLOT + turn
                req_ref[owner, pl.ds(turn, 1), :] = jnp.full((1, BLOCK), local, jnp.int32)

            @pl.when(k >= count[0])
            def _():
                slot_ref[k] = 0

            return carry

        lax.fori_loop(0, LMAX, put, 0)

    for part in range(PER_STEP // UNIT):
        rows = slice(part * UNIT, (part + 1) * UNIT)
        field = [g_ref[f, rows, :] for f in range(11)]
        shape = shape_of(center[0], center[1], *field)
        basis = basis_of(*field[:3])
        for f in range(6):
            out_ref[rows, f * BLOCK : (f + 1) * BLOCK] = shape[f]
        for ch in range(3):
            color = jnp.full((UNIT, BLOCK), 0.5, F32)
            for m in range(16):
                color = color + g_ref[11 + 3 * m + ch, rows, :] * basis[m]
            out_ref[rows, (6 + ch) * BLOCK : (7 + ch) * BLOCK] = color


def project_blocks(gaussians, ranks, count, order, place, center, peers):
    owned = gaussians.shape[1]
    smem = pl.BlockSpec(memory_space=pltpu.SMEM)
    return pl.pallas_call(
        functools.partial(project_kernel, owned, center),
        grid=(owned // PER_STEP,),
        in_specs=[smem, smem, smem, smem, pl.BlockSpec((FIELDS, PER_STEP, BLOCK), lambda i: (0, i, 0))],
        out_specs=[
            pl.BlockSpec((PER_STEP, WIDE), lambda i: (i, 0)),
            pl.BlockSpec((peers, SLOT, BLOCK), lambda i: (0, 0, 0)),
            smem,
        ],
        out_shape=[
            jax.ShapeDtypeStruct((owned, WIDE), F32),
            jax.ShapeDtypeStruct((peers, SLOT, BLOCK), jnp.int32),
            jax.ShapeDtypeStruct((LMAX,), jnp.int32),
        ],
        scratch_shapes=[pltpu.SMEM((peers,), jnp.int32)],
        name="project",
    )(ranks, count, order, place, gaussians)


def features():
    offset = np.arange(PIX)
    x = (offset % SIDE - SIDE // 2).astype(np.float32)
    y = (offset // SIDE - SIDE // 2).astype(np.float32)
    six = np.stack([np.ones_like(x), x, y, x * x, x * y, y * y])
    ahead = np.zeros((32, PIX), np.float32)
    for piece in range(3):
        ahead[6 * piece : 6 * piece + 6] = six
    back = np.zeros((16, PIX), np.float32)
    back[:6] = six
    return jnp.asarray(ahead, BF16), jnp.asarray(back, BF16)


def load_entries(slot_ref, recv_ref, ent_ref):
    for k in range(LMAX):
        slot = slot_ref[k]
        held = recv_ref[slot // SLOT, pl.ds(lax.rem(slot, SLOT) * NUMBERS, NUMBERS), :]
        ent_ref[pl.ds(k, NUMBERS, stride=LMAX), :] = held


def build_rows(place, count, ent_ref, field_ref, row_ref):
    mid_x = place[2].astype(F32)
    mid_y = place[1].astype(F32)
    mid_x = mid_x * SIDE + (SIDE // 2 + 0.5)
    mid_y = mid_y * SIDE + (SIDE // 2 + 0.5)
    field_ref[...] = jnp.zeros_like(field_ref)
    for unit in range(UNITS):
        u, v, a, b, c, log_o, r0, r1, r2 = [
            ent_ref[f * LMAX + unit * UNIT : f * LMAX + (unit + 1) * UNIT, :] for f in range(NUMBERS)
        ]
        entry = lax.broadcasted_iota(jnp.int32, (UNIT, BLOCK), 0) + unit * UNIT
        live = entry < count[0]
        du, dv = u - mid_x, v - mid_y
        k = -0.5 * LOG2E
        mix_u, mix_v = a * du + b * dv, b * du + c * dv
        coefs = [
            jnp.where(live, k * (mix_u * du + mix_v * dv) + LOG2E * log_o, -1e4),
            -2.0 * k * mix_u,
            -2.0 * k * mix_v,
            k * a,
            2.0 * k * b,
            k * c,
        ]
        coefs = coefs[:1] + [jnp.where(live, q, 0.0) for q in coefs[1:]]
        color = [jnp.where(live, r, 0.0) for r in (r0, r1, r2)]
        split = [pieces(q, 3) for q in coefs]
        shade = [pieces(r, 2) for r in color]
        columns = [split[f][piece] for piece in range(3) for f in range(6)]
        columns += [s[0] for s in shade] + [s[0] for s in shade] + [s[1] for s in shade]
        columns += color
        for f, column in enumerate(columns):
            field_ref[f * UNIT : (f + 1) * UNIT, :] = column
        for s in range(UNIT):
            table = field_ref[pl.ds(s, 32, stride=UNIT), :].T
            table = jnp.concatenate([table, jnp.zeros((BLOCK, BLOCK - 32), F32)], axis=1)
            row_ref[pl.ds(unit * ROWS + s, BLOCK, stride=UNIT), :] = table


def exponent_chunk(row_ref, ahead, chunk, alpha_ref):
    base = pl.multiple_of(chunk * CHUNK, CHUNK)
    rows = row_ref[pl.ds(base, CHUNK), :][:, :32].astype(BF16)
    alpha_ref[...] = jnp.exp2(jnp.dot(rows, ahead, preferred_element_type=F32))


def scan_chunk(row_ref, chunk, alpha_ref, carry):
    light, c0, c1, c2 = carry
    base = pl.multiple_of(chunk * CHUNK, CHUNK)
    for i in range(STEPS):
        alpha = alpha_ref[i * UNIT : (i + 1) * UNIT, :]
        shade = row_ref[pl.ds(base + i * UNIT, UNIT), :]
        weight = alpha * light
        light = light - weight
        c0 = c0 + shade[:, 27:28] * weight
        c1 = c1 + shade[:, 28:29] * weight
        c2 = c2 + shade[:, 29:30] * weight
    return light, c0, c1, c2


def forward_kernel(slot_ref, count, place, ahead_ref, recv_ref, image_ref, light_ref, color_ref,
                   row_ref, ent_ref, field_ref, even_ref, odd_ref):
    load_entries(slot_ref, recv_ref, ent_ref)
    build_rows(place, count, ent_ref, field_ref, row_ref)
    ahead = ahead_ref[...]
    last = UNITS * CHUNKS - 1
    exponent_chunk(row_ref, ahead, 0, even_ref)
    for unit in range(UNITS):
        zero = jnp.zeros((UNIT, PIX), F32)

        def advance(step, carry):
            chunk = unit * CHUNKS + 2 * step
            exponent_chunk(row_ref, ahead, chunk + 1, odd_ref)
            carry = scan_chunk(row_ref, chunk, even_ref, carry)
            exponent_chunk(row_ref, ahead, jnp.minimum(chunk + 2, last), even_ref)
            return scan_chunk(row_ref, chunk + 1, odd_ref, carry)

        light, c0, c1, c2 = lax.fori_loop(0, CHUNKS // 2, advance, (zero + 1.0, zero, zero, zero))
        rows = slice(unit * UNIT, (unit + 1) * UNIT)
        light_ref[rows, :] = light
        color_ref[0, rows, :] = c0
        color_ref[1, rows, :] = c1
        color_ref[2, rows, :] = c2
    light = jnp.ones((1, PIX), F32)
    image = [jnp.zeros((1, PIX), F32) for _ in range(3)]
    for k in range(LMAX):
        for ch in range(3):
            image[ch] = image[ch] + light * color_ref[ch, k : k + 1, :]
        light = light * light_ref[k : k + 1, :]
    for ch in range(3):
        for j in range(8):
            image_ref[ch, j : j + 1, :] = image[ch][:, j * BLOCK : (j + 1) * BLOCK]


def render(slots, count, place, ahead, recv):
    smem = pl.BlockSpec(memory_space=pltpu.SMEM)
    vmem = pl.BlockSpec(memory_space=pltpu.VMEM)
    return pl.pallas_call(
        forward_kernel,
        in_specs=[smem, smem, smem, vmem, vmem],
        out_specs=[vmem, vmem, vmem],
        out_shape=[
            jax.ShapeDtypeStruct((3, 8, BLOCK), F32),
            jax.ShapeDtypeStruct((LMAX, PIX), F32),
            jax.ShapeDtypeStruct((3, LMAX, PIX), F32),
        ],
        scratch_shapes=[
            VMEM((UNITS * ROWS, BLOCK), F32),
            VMEM((NUMBERS * LMAX, BLOCK), F32),
            VMEM((32 * UNIT, BLOCK), F32),
            VMEM((CHUNK, PIX), F32),
            VMEM((CHUNK, PIX), F32),
        ],
        name="render",
    )(slots, count, place, ahead, recv)


def long_row(ref, ch):
    return jnp.concatenate([ref[ch, j : j + 1, :] for j in range(8)], axis=1)


NT = (((1,), (1,)), ((), ()))


def backward_kernel(slot_ref, count, place, ahead_ref, back_ref, recv_ref, light_ref, color_ref, grad_ref,
                    out_ref, row_ref, ent_ref, field_ref, alpha_ref, weight_ref, shade_ref, start_ref,
                    behind_ref, moment_ref, result_ref):
    load_entries(slot_ref, recv_ref, ent_ref)
    build_rows(place, count, ent_ref, field_ref, row_ref)
    ahead = ahead_ref[...]
    grad = [long_row(grad_ref, ch) for ch in range(3)]
    high = [g.astype(BF16).astype(F32) for g in grad]
    low = [g - h for g, h in zip(grad, high)]
    zero = [jnp.zeros((1, PIX), F32)]
    mixed = jnp.concatenate(zero * 18 + high + low + high + zero * 5, axis=0).astype(BF16)
    tail = jnp.concatenate(zero * 8 + high + low + zero * 2, axis=0).astype(BF16)
    back = back_ref[...]

    light = jnp.ones((1, PIX), F32)
    for k in range(LMAX):
        start_ref[k : k + 1, :] = light
        light = light * light_ref[k : k + 1, :]
    behind = jnp.zeros((1, PIX), F32)
    for k in reversed(range(LMAX)):
        behind_ref[k : k + 1, :] = behind
        own = sum(grad[ch] * color_ref[ch, k : k + 1, :] for ch in range(3))
        behind = own + light_ref[k : k + 1, :] * behind

    def unit_pass(unit, carry):
        rows = pl.ds(pl.multiple_of(unit * UNIT, UNIT), UNIT)

        def recompute(chunk, light):
            base = pl.multiple_of(chunk * CHUNK, CHUNK)
            total = pl.multiple_of(unit * ROWS + base, CHUNK)
            packed = row_ref[pl.ds(total, CHUNK), :][:, :32].astype(BF16)
            alpha_ref[pl.ds(base, CHUNK), :] = jnp.exp2(jnp.dot(packed, ahead, preferred_element_type=F32))
            for i in range(STEPS):
                weight = alpha_ref[pl.ds(base + i * UNIT, UNIT), :] * light
                light = light - weight
                weight_ref[pl.ds(base + i * UNIT, UNIT), :] = weight
            return light

        lax.fori_loop(0, CHUNKS, recompute, start_ref[rows, :])

        def retreat(step, behind):
            base = pl.multiple_of((CHUNKS - 1 - step) * CHUNK, CHUNK)
            total = pl.multiple_of(unit * ROWS + base, CHUNK)
            packed = row_ref[pl.ds(total, CHUNK), :][:, :32].astype(BF16)
            shade_ref[...] = jnp.dot(packed, mixed, preferred_element_type=F32)
            for i in reversed(range(STEPS)):
                here = slice(i * UNIT, (i + 1) * UNIT)
                gap = shade_ref[here, :] - behind
                behind = behind + alpha_ref[pl.ds(base + i * UNIT, UNIT), :] * gap
                shade_ref[here, :] = weight_ref[pl.ds(base + i * UNIT, UNIT), :] * gap
            slope = shade_ref[...]
            weight = weight_ref[pl.ds(base, CHUNK), :]
            slope_high = slope.astype(BF16)
            slope_low = (slope - slope_high.astype(F32)).astype(BF16)
            weight_high = weight.astype(BF16)
            weight_low = (weight - weight_high.astype(F32)).astype(BF16)
            moment = lax.dot_general(slope_high, back, NT, preferred_element_type=F32)
            moment += lax.dot_general(slope_low, back, NT, preferred_element_type=F32)
            moment += lax.dot_general(weight_high, tail, NT, preferred_element_type=F32)
            moment += lax.dot_general(weight_low, tail, NT, preferred_element_type=F32)
            moment_ref[pl.ds(total, CHUNK), 0:16] = moment
            return behind

        lax.fori_loop(0, CHUNKS, retreat, behind_ref[rows, :])
        return carry

    moment_ref[...] = jnp.zeros_like(moment_ref)
    lax.fori_loop(0, UNITS, unit_pass, 0)

    mid_x = place[2].astype(F32) * SIDE + (SIDE // 2 + 0.5)
    mid_y = place[1].astype(F32) * SIDE + (SIDE // 2 + 0.5)
    for unit in range(UNITS):
        for s in range(UNIT):
            table = moment_ref[pl.ds(unit * ROWS + s, BLOCK, stride=UNIT), :].T
            field_ref[pl.ds(s, 16, stride=UNIT), :] = table[:16]
        m = [field_ref[f * UNIT : (f + 1) * UNIT, :] for f in range(14)]
        u, v, a, b, c = [ent_ref[f * LMAX + unit * UNIT : f * LMAX + (unit + 1) * UNIT, :] for f in range(5)]
        du, dv = u - mid_x, v - mid_y
        near_x, near_y = m[1] - du * m[0], m[2] - dv * m[0]
        values = [
            a * near_x + b * near_y,
            b * near_x + c * near_y,
            -0.5 * (m[3] - du * (m[1] + near_x)),
            -(m[4] - du * m[2] - dv * near_x),
            -0.5 * (m[5] - dv * (m[2] + near_y)),
            m[0],
            m[8] + m[11],
            m[9] + m[12],
            m[10] + m[13],
        ]
        for f, value in enumerate(values):
            result_ref[f * LMAX + unit * UNIT : f * LMAX + (unit + 1) * UNIT, :] = value
    for k in range(LMAX):

        @pl.when(k < count[0])
        def _():
            slot = slot_ref[k]
            row = pl.ds(lax.rem(slot, SLOT) * NUMBERS, NUMBERS)
            out_ref[slot // SLOT, row, :] = result_ref[pl.ds(k, NUMBERS, stride=LMAX), :]


def render_gradient(slots, count, place, ahead, back, recv, light, color, grad):
    smem = pl.BlockSpec(memory_space=pltpu.SMEM)
    vmem = pl.BlockSpec(memory_space=pltpu.VMEM)
    return pl.pallas_call(
        backward_kernel,
        in_specs=[smem, smem, smem] + [vmem] * 6,
        out_specs=vmem,
        out_shape=jax.ShapeDtypeStruct(recv.shape, F32),
        scratch_shapes=[
            VMEM((UNITS * ROWS, BLOCK), F32),
            VMEM((NUMBERS * LMAX, BLOCK), F32),
            VMEM((32 * UNIT, BLOCK), F32),
            VMEM((ROWS, PIX), F32),
            VMEM((ROWS, PIX), F32),
            VMEM((CHUNK, PIX), F32),
            VMEM((LMAX, PIX), F32),
            VMEM((LMAX, PIX), F32),
            VMEM((UNITS * ROWS, BLOCK), F32),
            VMEM((NUMBERS * LMAX, BLOCK), F32),
        ],
        name="render_gradient",
    )(slots, count, place, ahead, back, recv, light, color, grad)


def pull_kernel(center, scale, req_ref, back_ref, total_ref, g_ref, out_ref, loss_ref, dense_ref):
    step = pl.program_id(0)

    @pl.when(step == 0)
    def _():
        loss_ref[0] = jnp.sum(total_ref[...]) * scale
        owned = dense_ref.shape[0]
        req = jnp.concatenate([req_ref[:, turn, :] for turn in range(CAP)], axis=0)
        lane = lax.broadcasted_iota(jnp.int32, req.shape, 1)
        chosen = jnp.where(req == lane, 1.0, 0.0).T[:owned].astype(BF16)
        asked = req >= 0
        for f in range(NUMBERS):
            cols = slice(f * BLOCK, (f + 1) * BLOCK)
            value = jnp.concatenate([back_ref[:, turn * NUMBERS + f, :] for turn in range(CAP)], axis=0)
            value = jnp.where(asked, value, 0.0)
            dense_ref[:, cols] = sum(
                jnp.dot(chosen, part.astype(BF16), preferred_element_type=F32) for part in pieces(value, 3)
            )

    for part in range(PER_STEP // UNIT):
        here = slice(part * UNIT, (part + 1) * UNIT)
        rows = pl.ds(pl.multiple_of(step * PER_STEP + part * UNIT, UNIT), UNIT)
        cot = [dense_ref[rows, f * BLOCK : (f + 1) * BLOCK] for f in range(9)]
        field = [g_ref[f, here, :] for f in range(11)]
        _, pull = jax.vjp(functools.partial(shape_of, center[0], center[1]), *field)
        grads = list(pull(tuple(cot[:6])))
        basis, pull_basis = jax.vjp(basis_of, *field[:3])
        basis_cot = []
        for m in range(16):
            total = jnp.zeros((UNIT, BLOCK), F32)
            for ch in range(3):
                total = total + g_ref[11 + 3 * m + ch, here, :] * cot[6 + ch]
                out_ref[11 + 3 * m + ch, here, :] = basis[m] * cot[6 + ch]
            basis_cot.append(total)
        extra = pull_basis(basis_cot)
        for f in range(3):
            grads[f] = grads[f] + extra[f]
        for f in range(11):
            out_ref[f, here, :] = grads[f]


def pull_blocks(req, back, total, gaussians, center, scale):
    owned = gaussians.shape[1]
    return pl.pallas_call(
        functools.partial(pull_kernel, center, scale),
        grid=(owned // PER_STEP,),
        in_specs=[
            pl.BlockSpec(req.shape, lambda i: (0, 0, 0)),
            pl.BlockSpec(back.shape, lambda i: (0, 0, 0)),
            pl.BlockSpec(total.shape, lambda i: (0, 0)),
            pl.BlockSpec((FIELDS, PER_STEP, BLOCK), lambda i: (0, i, 0)),
        ],
        out_specs=[
            pl.BlockSpec((FIELDS, PER_STEP, BLOCK), lambda i: (0, i, 0)),
            pl.BlockSpec(memory_space=pltpu.SMEM),
        ],
        out_shape=[
            jax.ShapeDtypeStruct(gaussians.shape, F32),
            jax.ShapeDtypeStruct((1,), F32),
        ],
        scratch_shapes=[VMEM((owned, WIDE), F32)],
        name="pull",
    )(req, back, total, gaussians)


MESH = pl.DeviceIdType.MESH
NEAR = [(dy, dx) for dy in (-1, 0, 1) for dx in (-1, 0, 1) if (dy, dx) != (0, 0)]


def greet(targets):
    barrier = pltpu.get_barrier_semaphore()
    for target in targets:
        pl.semaphore_signal(barrier, inc=1, device_id=target, device_id_type=MESH)
    pl.semaphore_wait(barrier, len(targets))


def row_peers(n):
    me = lax.axis_index("tx")
    return me, [lax.rem(me + d, n) for d in range(1, n)]


def serve_kernel(n, req_ref, table_ref, asked_ref, recv_ref, served_ref, req_send, req_recv, data_send, data_recv):
    me, peers = row_peers(n)
    greet([{"tx": peer} for peer in peers])
    asks = []
    for d, peer in enumerate(peers):
        asks.append(
            pltpu.make_async_remote_copy(
                src_ref=req_ref.at[peer],
                dst_ref=asked_ref.at[me],
                send_sem=req_send.at[d],
                recv_sem=req_recv.at[d],
                device_id={"tx": peer},
                device_id_type=MESH,
            )
        )
        asks[-1].start()
    asked_ref[me] = req_ref[me]
    parts = [part.astype(BF16) for part in pieces(table_ref[...], 3)]
    for copy in asks:
        copy.wait_recv()
    owned = table_ref.shape[0]
    asked = jnp.concatenate([asked_ref[:, turn, :] for turn in range(CAP)], axis=0)
    lane = lax.broadcasted_iota(jnp.int32, asked.shape, 1)
    chosen = jnp.where(asked == lane, 1.0, 0.0)[:, :owned].astype(BF16)
    served = sum(jnp.dot(chosen, part, preferred_element_type=F32) for part in parts)
    for turn in range(CAP):
        for f in range(NUMBERS):
            value = served[turn * n : (turn + 1) * n, f * BLOCK : (f + 1) * BLOCK]
            served_ref[:, turn * NUMBERS + f, :] = value
    sends = []
    for d, peer in enumerate(peers):
        sends.append(
            pltpu.make_async_remote_copy(
                src_ref=served_ref.at[peer],
                dst_ref=recv_ref.at[me],
                send_sem=data_send.at[d],
                recv_sem=data_recv.at[d],
                device_id={"tx": peer},
                device_id_type=MESH,
            )
        )
        sends[-1].start()
    recv_ref[me] = served_ref[me]
    for copy in sends:
        copy.wait_recv()
    for copy in asks:
        copy.wait_send()
    for copy in sends:
        copy.wait_send()


def serve(req, table, n):
    vmem = pl.BlockSpec(memory_space=pltpu.VMEM)
    dma = pltpu.SemaphoreType.DMA((n - 1,))
    return pl.pallas_call(
        functools.partial(serve_kernel, n),
        in_specs=[vmem, vmem],
        out_specs=[vmem, vmem],
        out_shape=[
            jax.ShapeDtypeStruct(req.shape, jnp.int32),
            jax.ShapeDtypeStruct((n, PACK, BLOCK), F32),
        ],
        scratch_shapes=[VMEM((n, PACK, BLOCK), F32), dma, dma, dma, dma],
        compiler_params=pltpu.CompilerParams(collective_id=0, has_side_effects=True),
        name="serve",
    )(req, table)


def reply_kernel(n, rows, grad_ref, part_ref, back_ref, total_ref, column_ref, sum_ref, line_ref,
                 data_send, data_recv, col_send, col_recv, row_send, row_recv):
    me, peers = row_peers(n)
    mine = lax.axis_index("ty")
    others = [lax.rem(mine + d, rows) for d in range(1, rows)]
    greet([{"tx": peer} for peer in peers] + [{"ty": other} for other in others])
    columns = []
    for d, other in enumerate(others):
        columns.append(
            pltpu.make_async_remote_copy(
                src_ref=part_ref,
                dst_ref=column_ref.at[mine],
                send_sem=col_send.at[d],
                recv_sem=col_recv.at[d],
                device_id={"ty": other},
                device_id_type=MESH,
            )
        )
        columns[-1].start()
    sends = []
    for d, peer in enumerate(peers):
        sends.append(
            pltpu.make_async_remote_copy(
                src_ref=grad_ref.at[peer],
                dst_ref=back_ref.at[me],
                send_sem=data_send.at[d],
                recv_sem=data_recv.at[d],
                device_id={"tx": peer},
                device_id_type=MESH,
            )
        )
        sends[-1].start()
    column_ref[mine] = part_ref[...]
    back_ref[me] = grad_ref[me]
    for copy in columns:
        copy.wait_recv()
    sum_ref[...] = sum(column_ref[r] for r in range(rows))
    lines = []
    for d, peer in enumerate(peers):
        lines.append(
            pltpu.make_async_remote_copy(
                src_ref=sum_ref,
                dst_ref=line_ref.at[me],
                send_sem=row_send.at[d],
                recv_sem=row_recv.at[d],
                device_id={"tx": peer},
                device_id_type=MESH,
            )
        )
        lines[-1].start()
    line_ref[me] = sum_ref[...]
    for copy in lines:
        copy.wait_recv()
    total_ref[...] = sum(line_ref[c] for c in range(n))
    for copy in sends:
        copy.wait_recv()
    for copy in columns + sends + lines:
        copy.wait_send()


def reply(grads, part, n, rows):
    vmem = pl.BlockSpec(memory_space=pltpu.VMEM)
    wide = pltpu.SemaphoreType.DMA((n - 1,))
    tall = pltpu.SemaphoreType.DMA((rows - 1,))
    return pl.pallas_call(
        functools.partial(reply_kernel, n, rows),
        in_specs=[vmem, vmem],
        out_specs=[vmem, vmem],
        out_shape=[
            jax.ShapeDtypeStruct(grads.shape, F32),
            jax.ShapeDtypeStruct(part.shape, F32),
        ],
        scratch_shapes=[
            VMEM((rows,) + part.shape, F32),
            VMEM(part.shape, F32),
            VMEM((n,) + part.shape, F32),
            wide,
            wide,
            tall,
            tall,
            wide,
            wide,
        ],
        compiler_params=pltpu.CompilerParams(collective_id=1, has_side_effects=True),
        name="reply",
    )(grads, part)


def window_taps():
    offsets = np.arange(11, dtype=np.float32) - np.float32(5.0)
    taps = np.exp(-offsets * offsets / np.float32(4.5))
    return [float(tap) for tap in taps / np.sum(taps)]


def similarity(mean_a, mean_b, square_a, square_b, cross):
    var_a = square_a - mean_a * mean_a
    var_b = square_b - mean_b * mean_b
    covar = cross - mean_a * mean_b
    top = (2.0 * mean_a * mean_b + LUMA_TERM) * (2.0 * covar + CONTRAST_TERM)
    bottom = (mean_a * mean_a + mean_b * mean_b + LUMA_TERM) * (var_a + var_b + CONTRAST_TERM)
    return top / bottom


EXT = 3 * SIDE
TOP = SIDE - 8
TALL = SIDE + 16


def symmetric(taps, part):
    total = taps[5] * part(5)
    for k in range(5):
        total = total + taps[k] * (part(k) + part(10 - k))
    return total


def filter_rows(taps, ref, start, rows):
    tall = symmetric(taps, lambda k: ref[start + k : start + k + rows, :])
    return symmetric(taps, lambda k: tall if k == 5 else pltpu.roll(tall, (5 - k) % BLOCK, 1))


def similarity_kernel(cols, rows, image_ref, goal_ref, grad_ref, part_ref, near_ref, pic_ref, aim_ref,
                      prod_ref, coef_ref, flat_ref, image_send, image_recv, goal_send, goal_recv):
    row, col = lax.axis_index("ty"), lax.axis_index("tx")
    targets = [
        {"ty": lax.rem(row + dy + rows, rows), "tx": lax.rem(col + dx + cols, cols)} for dy, dx in NEAR
    ]
    greet(targets)
    copies = []
    for d, target in enumerate(targets):
        for src, half, send, recv in (
            (image_ref, 0, image_send, image_recv),
            (goal_ref, 1, goal_send, goal_recv),
        ):
            copies.append(
                pltpu.make_async_remote_copy(
                    src_ref=src,
                    dst_ref=near_ref.at[d, half],
                    send_sem=send.at[d],
                    recv_sem=recv.at[d],
                    device_id=target,
                    device_id_type=MESH,
                )
            )
            copies[-1].start()
    lane = lax.broadcasted_iota(jnp.int32, (8, BLOCK), 1)
    wide = lane + (col - 1) * SIDE
    inside = (wide >= 0) & (wide < cols * SIDE) & (lane < EXT)
    for copy in copies:
        copy.wait_recv()
    for dy in (-1, 0, 1):
        high = jnp.zeros((8, BLOCK), jnp.int32) + (row + dy)
        there = inside & (high >= 0) & (high < rows)
        for half, own, out in ((0, image_ref, pic_ref), (1, goal_ref, aim_ref)):
            for ch in range(3):
                tiles = []
                for dx in (-1, 0, 1):
                    if (dy, dx) == (0, 0):
                        tiles.append(own[ch])
                    else:
                        tiles.append(near_ref[NEAR.index((-dy, -dx)), half, ch])
                for q in range(4):
                    moved = []
                    for place, tile in enumerate(tiles):
                        shift = (SIDE * (place - q)) % BLOCK
                        moved.append(pltpu.roll(tile, shift, 1) if shift else tile)
                    value = jnp.where(lane < SIDE, moved[0], jnp.where(lane < 2 * SIDE, moved[1], moved[2]))
                    value = jnp.where(there, value, 0.0)
                    out[pl.ds(ch * EXT + (dy + 1) * SIDE + q, 8, stride=4), :] = value
    taps = window_taps()
    high = lax.broadcasted_iota(jnp.int32, (TALL, BLOCK), 0) + (row * SIDE + TOP - SIDE)
    long = lax.broadcasted_iota(jnp.int32, (TALL, BLOCK), 1) + (col - 1) * SIDE
    scored = (high >= 0) & (high < rows * SIDE) & (long >= 0) & (long < cols * SIDE)
    middle = lax.broadcasted_iota(jnp.int32, (SIDE, BLOCK), 1)
    middle = (middle >= SIDE) & (middle < 2 * SIDE)
    part = jnp.zeros((SIDE, BLOCK), F32)
    for ch in range(3):
        base = ch * EXT
        picture = pic_ref[base : base + EXT, :]
        goal = aim_ref[base : base + EXT, :]
        prod_ref[0:EXT, :] = picture * picture
        prod_ref[EXT : 2 * EXT, :] = goal * goal
        prod_ref[2 * EXT : 3 * EXT, :] = picture * goal
        maps = [
            filter_rows(taps, ref, start + TOP - 5, TALL)
            for ref, start in (
                (pic_ref, base),
                (aim_ref, base),
                (prod_ref, 0),
                (prod_ref, EXT),
                (prod_ref, 2 * EXT),
            )
        ]
        score, pull_score = jax.vjp(similarity, *maps)
        parts = pull_score(jnp.full_like(score, -STRUCT_WEIGHT))
        for i, which in enumerate((0, 2, 4)):
            coef_ref[i * TALL : (i + 1) * TALL, :] = jnp.where(scored, parts[which], 0.0)
        smooth = [filter_rows(taps, coef_ref, i * TALL + SIDE - TOP - 5, SIDE) for i in range(3)]
        image = pic_ref[base + SIDE : base + 2 * SIDE, :]
        target = aim_ref[base + SIDE : base + 2 * SIDE, :]
        gap = image - target
        robust = jnp.sqrt(gap * gap + ROBUST_TERM)
        own_score = score[SIDE - TOP : 2 * SIDE - TOP, :]
        part = part + (1.0 - STRUCT_WEIGHT) * robust + STRUCT_WEIGHT * (1.0 - own_score)
        flat_ref[...] = (
            smooth[0]
            + 2.0 * image * smooth[1]
            + target * smooth[2]
            + (1.0 - STRUCT_WEIGHT) * gap / robust
        )
        value = jnp.zeros((8, BLOCK), F32)
        for q in range(4):
            line = flat_ref[pl.ds(q, 8, stride=4), :]
            shift = (SIDE * (q - 1)) % BLOCK
            line = pltpu.roll(line, shift, 1) if shift else line
            value = jnp.where((lane >= SIDE * q) & (lane < SIDE * (q + 1)), line, value)
        grad_ref[ch] = value
    part = jnp.where(middle, part, 0.0)
    part_ref[...] = part[0:8] + part[8:16] + part[16:24] + part[24:32]
    for copy in copies:
        copy.wait_send()


def image_gradient(image, goal, cols, rows):
    vmem = pl.BlockSpec(memory_space=pltpu.VMEM)
    dma = pltpu.SemaphoreType.DMA((len(NEAR),))
    return pl.pallas_call(
        functools.partial(similarity_kernel, cols, rows),
        in_specs=[vmem, vmem],
        out_specs=[vmem, vmem],
        out_shape=[jax.ShapeDtypeStruct(image.shape, F32), jax.ShapeDtypeStruct((8, BLOCK), F32)],
        scratch_shapes=[
            VMEM((len(NEAR), 2) + image.shape, F32),
            VMEM((3 * EXT, BLOCK), F32),
            VMEM((3 * EXT, BLOCK), F32),
            VMEM((3 * EXT, BLOCK), F32),
            VMEM((3 * TALL, BLOCK), F32),
            VMEM((SIDE, BLOCK), F32),
            dma,
            dma,
            dma,
            dma,
        ],
        compiler_params=pltpu.CompilerParams(collective_id=2, has_side_effects=True),
        name="image_gradient",
    )(image, goal)


def per_device(gaussians, tile_lists, tile_counts, depth_order, target):
    across = lax.axis_size("tx")
    down = lax.axis_size("ty")
    row_index = lax.axis_index("ty")
    col_index = lax.axis_index("tx")
    height = SIDE * down
    width = SIDE * across
    center = (0.5 * width, 0.5 * height)
    ranks = tile_lists.reshape(LMAX)
    count = tile_counts.reshape(1)
    place = jnp.stack([row_index * across, row_index, col_index]).astype(jnp.int32)
    by_field = gaussians.transpose(1, 0, 2)
    table, req, slots = project_blocks(by_field, ranks, count, depth_order, place, center, across)
    asked, recv = serve(req, table, across)
    ahead, back = features()
    image, light, color = render(slots, count, place, ahead, recv)
    image_grad, part = image_gradient(image, target.reshape(3, 8, BLOCK), across, down)
    grads = render_gradient(slots, count, place, ahead, back, recv, light, color, image_grad)
    returned, total = reply(grads, part, across, down)
    pulled, loss = pull_blocks(asked, returned, total, by_field, center, 1.0 / (3.0 * height * width))
    return pulled.transpose(1, 0, 2), loss.reshape(())


def solution(mesh):
    return jax.shard_map(
        per_device,
        mesh=mesh,
        in_specs=(
            P(("ty", "tx"), None, None),
            P("ty", "tx", None),
            P("ty", "tx"),
            P(),
            P(None, "ty", "tx"),
        ),
        out_specs=(P(("ty", "tx"), None, None), P()),
        check_vma=False,
    )
```
